128 devices in a mesh: cell: 32 (over x, z, y_hi), spec: 4 (over y_lo, core).
Axes of the slice: x: 4, y: 4 (y_hi: 2, y_lo: 2; y = y_hi * 2 + y_lo), z: 4, core: 2. Of those that a mesh axis runs over, the one named last changes fastest.
Arguments:
- fields: bfloat16 [4, 1024, 384], P('spec', 'cell'), may hold values from -6 to 6
- tensors: bfloat16 [16, 384, 384, 384], P('spec', 'cell'), may hold values from -0.0078125 to 0.0078125
- pair_table: int32 [4, 4], replicated, may hold values from 0 to 15, as said below
- plus_flux: float32 [4, 384, 384], P('spec'), may hold values from -0.3125 to 0.3125
- minus_flux: float32 [4, 384, 384], P('spec'), may hold values from -0.3125 to 0.3125
- face_limiter: int32 [4, 1024], P('spec', 'cell'), may hold values from 0 to 2
Outputs:
- new_field: float32 [4, 1024, 384], P('spec', 'cell')
- collision: float32 [4, 1024, 384], P('spec', 'cell')
The draws below stay inside these ranges and needn't reach their ends.
Inputs may be any that keep to these rules, and one draw needn't show every extreme that they name: Row s of pair_table names each of the tensors s * 4 to s * 4 + 3 exactly once. `face_limiter`: 0 first order, 1 minmod slope, 2 monotonized central slope.
All inputs are finite; a program needn't handle non-finite values.
Results may differ from the reference program's by a relative error of at most 0.0004.
Values may be sent and summed in bfloat16 or wider, within the bound.
A program may use at most 64 MiB of HBM per device.

```python
import math
import jax
import jax.numpy as jnp
from jax import lax

M = 384
SPEC = 4
NPAIR = 16
NCELL = 1024


def draw_pair_table(key, part):
    keys = jax.random.split(jax.random.fold_in(key, 17), SPEC)
    orders = jax.vmap(lambda single: jax.random.permutation(single, SPEC))(keys)
    base = jnp.arange(SPEC, dtype=jnp.int32)[:, None] * SPEC
    return (base + orders.astype(jnp.int32)).astype(jnp.int32)


def touch_ends(entries, rng, low, high):
    longest = entries.shape.index(max(entries.shape))
    spots = []
    for shift in (0, 1):
        where = [jax.random.randint(jax.random.fold_in(rng, axis), (), 0, length) for axis, length in enumerate(entries.shape)]
        where[longest] = (where[longest] + shift) % entries.shape[longest]
        spots.append(tuple(where))
    return entries.at[spots[0]].set(low).at[spots[1]].set(high)


def block_scale(own_key, dims, shards, low, high):
    def one(position, parts):
        steps = jax.random.uniform(jax.random.fold_in(jax.random.fold_in(own_key, 6), position), (parts,), jnp.float32, low / len(shards), high / len(shards))
        return jnp.repeat(jnp.exp(steps), dims[position] // parts).reshape((-1,) + (1,) * (len(dims) - position - 1))

    gain = one(*shards[0])
    for cut in shards[1:]:
        gain = gain * one(*cut)
    return gain


def gaussian(own_key, shape, scale, reach, shards=(), held_as=jnp.bfloat16):
    entries = jax.random.normal(own_key, shape, jnp.float32) * scale
    if len(shards) > 0:
        entries = block_scale(own_key, shape, shards, -0.22, 0.18) * entries
    return jnp.clip(entries, min=-reach, max=reach).astype(held_as)


def setup_inputs(seed: int = 0) -> dict:
    streams_of = jax.random.split(jax.random.key(seed), 7)
    fields = gaussian(streams_of[0], (SPEC, NCELL, M), 1.0, 6.0, ((0, 4), (1, 32)))
    tensors = gaussian(streams_of[1], (NPAIR, M, M, M), (SPEC * M * M) ** -0.5, 0.0078125, ((0, 4), (1, 32)))
    pair_table = draw_pair_table(jax.random.fold_in(streams_of[6], 71), 0)
    plus_flux = gaussian(streams_of[3], (SPEC, M, M), M ** -0.5, 0.3125, ((0, 4),), jnp.float32)
    minus_flux = gaussian(streams_of[4], (SPEC, M, M), M ** -0.5, 0.3125, ((0, 4),), jnp.float32)
    face_limiter = touch_ends(jax.random.randint(streams_of[5], (SPEC, NCELL), 0, 3), jax.random.fold_in(streams_of[5], 1), 0, 2).astype(jnp.int32)
    return dict(fields=fields, tensors=tensors, pair_table=pair_table, plus_flux=plus_flux, minus_flux=minus_flux, face_limiter=face_limiter)


def minmod_two(first, second):
    return jnp.where(first * second > 0, jnp.sign(first) * jnp.minimum(jnp.abs(first), jnp.abs(second)), 0.0)


def minmod_three(first, second, third):
    same = (first * second > 0) & (second * third > 0)
    least = jnp.minimum(jnp.minimum(jnp.abs(first), jnp.abs(second)), jnp.abs(third))
    return jnp.where(same, jnp.sign(first) * least, 0.0)


def collide(fields, tensors, pair_table):
    block = math.gcd(NCELL, 32)
    field32 = fields.astype(jnp.float32)
    blocked = field32.reshape(SPEC, NCELL // block, block, M)
    results = []
    for owner in range(SPEC):
        total = jnp.zeros((NCELL // block, block, M), jnp.float32)
        for partner in range(SPEC):
            tensor = lax.dynamic_index_in_dim(tensors, pair_table[owner, partner], 0, keepdims=False).astype(jnp.float32)

            def one_block(pieces):
                own_piece, partner_piece = pieces
                inner = jnp.einsum("cj,kij->cki", partner_piece, tensor)
                return jnp.einsum("cki,ci->ck", inner, own_piece)

            total = total + lax.map(one_block, (blocked[owner], blocked[partner]))
        results.append(total.reshape(NCELL, M))
    return jnp.stack(results)


def reference(fields, tensors, pair_table, plus_flux, minus_flux, face_limiter):
    collision = collide(fields, tensors, pair_table)
    field32 = fields.astype(jnp.float32)
    before = jnp.roll(field32, 1, axis=1)
    after = jnp.roll(field32, -1, axis=1)
    lower = field32 - before
    upper = after - field32
    slope_one = minmod_two(lower, upper)
    slope_two = minmod_three(2.0 * lower, 0.5 * (lower + upper), 2.0 * upper)
    flags = face_limiter[:, :, None]
    zero = jnp.zeros_like(slope_one)
    here = jnp.where(flags == 1, slope_one, jnp.where(flags == 2, slope_two, zero))
    slope_one_next = jnp.roll(slope_one, -1, axis=1)
    slope_two_next = jnp.roll(slope_two, -1, axis=1)
    there = jnp.where(flags == 1, slope_one_next, jnp.where(flags == 2, slope_two_next, zero))
    left_state = field32 + 0.5 * here
    right_state = after - 0.5 * there
    flux = jnp.einsum("scm,smn->scn", left_state, plus_flux, precision=lax.Precision.HIGHEST)
    flux = flux + jnp.einsum("scm,smn->scn", right_state, minus_flux, precision=lax.Precision.HIGHEST)
    new_field = field32 + 0.4 * (jnp.roll(flux, 1, axis=1) - flux) + 0.5 * collision
    return new_field, collision
```

```python
import functools

import jax
import jax.numpy as jnp
from jax import lax
from jax.experimental import pallas as pl
from jax.experimental.pallas import tpu as pltpu
from jax.sharding import PartitionSpec as P

MESH = pl.DeviceIdType.MESH
HALF = 16
GROUP = 4


def minmod_two(first, second):
    least = jnp.minimum(jnp.abs(first), jnp.abs(second))
    return jnp.where(first * second > 0, jnp.where(first > 0, least, -least), 0.0)


def minmod_three(first, second, third):
    same = (first * second > 0) & (second * third > 0)
    least = jnp.minimum(jnp.minimum(jnp.abs(first), jnp.abs(second)), jnp.abs(third))
    return jnp.where(same, jnp.where(first > 0, least, -least), 0.0)


def mod(value, size):
    return lax.rem(value, size)


def step_kernel(
    dims,
    pair_table,
    fields,
    tensors,
    plus_hbm,
    minus_hbm,
    limiter,
    new_ref,
    coll_ref,
    held0,
    held1,
    held2,
    held3,
    a_ref,
    plus_ref,
    minus_ref,
    flag_ref,
    prior_flag,
    before,
    after,
    own_t,
    line,
    outgoing,
    incoming,
    rows,
    base,
    load_sem,
    edge_send,
    edge_recv,
    x_send,
    x_recv,
    line_send,
    line_recv,
    pair_send,
    pair_recv,
    exit_send,
    exit_recv,
):
    nx, nz, nyh, nyl, ncore = dims
    ny = nyh * nyl
    held = (held0, held1, held2, held3)
    species = nyl * ncore
    out_modes = tensors.shape[1]
    modes = tensors.shape[2]
    plane = nz * nyh
    cell = lax.axis_index("cell")
    spec = lax.axis_index("spec")
    yh = mod(cell, nyh)
    z = mod(lax.div(cell, nyh), nz)
    x = lax.div(cell, plane)
    spot = mod(cell, plane)
    yl = lax.div(spec, ncore)
    core = mod(spec, ncore)
    y = yh * nyl + yl

    def device(x_at, z_at, y_at, core_at):
        return (
            (x_at * nz + z_at) * nyh + lax.div(y_at, nyl),
            mod(y_at, nyl) * ncore + core_at,
        )

    def remote(src, dst, send, recv, to):
        return pltpu.make_async_remote_copy(
            src_ref=src,
            dst_ref=dst,
            send_sem=send,
            recv_sem=recv,
            device_id=to,
            device_id_type=MESH,
        )

    def block(q):
        return held[q].at[core, yl, z, yh]

    loads = [
        pltpu.make_async_copy(tensors.at[p], a_ref.at[p], load_sem.at[p])
        for p in range(species)
    ]
    own_load = pltpu.make_async_copy(fields.at[0], block(0), load_sem.at[4])
    flag_load = pltpu.make_async_copy(limiter, flag_ref, load_sem.at[5])
    plus_load = pltpu.make_async_copy(plus_hbm.at[0], plus_ref, load_sem.at[6])
    minus_load = pltpu.make_async_copy(minus_hbm.at[0], minus_ref, load_sem.at[7])
    own_load.start()
    flag_load.start()
    plus_load.start()
    minus_load.start()
    for load in loads:
        load.start()

    ring = nx * plane
    succ = (mod(cell + 1, ring), spec)
    pred = (mod(cell + ring - 1, ring), spec)
    greeted = [device(x, z, y, 1 - core), succ, pred]
    greeted += [device(mod(x + o, nx), z, y, core) for o in range(1, nx)]
    greeted += [device(x, mod(z + o, nz), y, core) for o in range(1, nz)]
    greeted += [device(x, z, mod(y + o, ny), core) for o in range(1, ny)]
    barrier = pltpu.get_barrier_semaphore()
    for other in greeted:
        pl.semaphore_signal(barrier, inc=1, device_id=other, device_id_type=MESH)
    own_load.wait()
    flag_load.wait()
    pl.semaphore_wait(barrier, len(greeted))

    def first(q):
        copies = []
        for o in range(1, ny):
            here = held[q].at[core, yl, z, yh, 0]
            to = device(x, z, mod(y + o, ny), core)
            copies.append((here, here, line_send.at[q, o - 1], line_recv.at[q, o - 1], to))
        for o in range(1, nz):
            here = held[q].at[core, yl, z, yh, 1]
            to = device(x, mod(z + o, nz), y, core)
            copies.append((here, here, line_send.at[q, o + 2], line_recv.at[q, o + 2], to))
        return [remote(*c) for c in copies]

    def second(q):
        copies = []
        for o in range(1, nz):
            here = held[q].at[core, :, z, :, 0]
            to = device(x, mod(z + o, nz), y, core)
            copies.append((here, here, line_send.at[q, o + 5], line_recv.at[q, o + 5], to))
        for o in range(1, ny):
            here = held[q].at[core, yl, :, yh, 1]
            to = device(x, z, mod(y + o, ny), core)
            copies.append((here, here, line_send.at[q, o + 8], line_recv.at[q, o + 8], to))
        return [remote(*c) for c in copies]

    def first_in(q):
        me = (cell, spec)
        for o in range(1, ny):
            y_from = mod(y + ny - o, ny)
            there = held[q].at[core, mod(y_from, nyl), z, lax.div(y_from, nyl), 0]
            remote(there, there, line_send.at[q, o - 1], line_recv.at[q, o - 1], me).wait_recv()
        for o in range(1, nz):
            there = held[q].at[core, yl, mod(z + nz - o, nz), yh, 1]
            remote(there, there, line_send.at[q, o + 2], line_recv.at[q, o + 2], me).wait_recv()

    def second_in(q):
        me = (cell, spec)
        for o in range(1, nz):
            there = held[q].at[core, :, mod(z + nz - o, nz), :, 0]
            remote(there, there, line_send.at[q, o + 5], line_recv.at[q, o + 5], me).wait_recv()
        for o in range(1, ny):
            y_from = mod(y + ny - o, ny)
            there = held[q].at[core, mod(y_from, nyl), :, lax.div(y_from, nyl), 1]
            remote(there, there, line_send.at[q, o + 8], line_recv.at[q, o + 8], me).wait_recv()

    def paired(q, which):
        half = held[q].at[which]
        return remote(half, half, pair_send.at[q], pair_recv.at[q], device(x, z, y, 1 - core))

    sent = []

    def go(copies):
        for copy in copies:
            copy.start()
        sent.extend(copies)

    go(
        [
            remote(held[0].at[core, yl, z, yh, 1], before, edge_send.at[0], edge_recv.at[0], succ),
            remote(held[0].at[core, yl, z, yh, 0], after, edge_send.at[1], edge_recv.at[1], pred),
            remote(flag_ref, prior_flag, edge_send.at[2], edge_recv.at[2], succ),
        ]
    )
    go(first(0))
    order = (2, 1, 3)
    go(
        [
            remote(block(0), block(q), x_send.at[q], x_recv.at[q], device(mod(x + nx - q, nx), z, y, core))
            for q in order
        ]
    )
    first_in(0)
    go(second(0))

    me = (cell, spec)
    plus_load.wait()
    minus_load.wait()
    remote(before, before, edge_send.at[0], edge_recv.at[0], me).wait_recv()
    remote(after, after, edge_send.at[1], edge_recv.at[1], me).wait_recv()
    remote(flag_ref, prior_flag, edge_send.at[2], edge_recv.at[2], me).wait_recv()
    own = held[0][core, yl, z, yh].reshape(2 * HALF, modes)
    wide = jnp.concatenate([before[...], own, after[...]], axis=0).astype(jnp.float32)
    count = 4 * HALF
    up = pltpu.roll(wide, 1, 0)
    down = pltpu.roll(wide, count - 1, 0)
    lower = wide - up
    upper = down - wide
    slope_one = minmod_two(lower, upper)
    slope_two = minmod_three(2.0 * lower, 0.5 * (lower + upper), 2.0 * upper)
    line[...] = jnp.zeros_like(line)
    line[0:1, 0 : 2 * HALF] = flag_ref[...].astype(jnp.float32)
    line[1:2, 0 : 2 * HALF] = prior_flag[...].astype(jnp.float32)
    columns = jnp.transpose(line[...])
    flags = jnp.concatenate(
        [
            columns[HALF : 2 * HALF, 1:2],
            columns[0 : 2 * HALF, 0:1],
            jnp.zeros((HALF, 1), jnp.float32),
        ],
        axis=0,
    )
    flags = jnp.broadcast_to(flags, (count, modes))
    here = jnp.where(flags == 1.0, slope_one, jnp.where(flags == 2.0, slope_two, 0.0))
    next_one = pltpu.roll(slope_one, count - 1, 0)
    next_two = pltpu.roll(slope_two, count - 1, 0)
    there = jnp.where(flags == 1.0, next_one, jnp.where(flags == 2.0, next_two, 0.0))
    left_state = (wide + 0.5 * here)[0 : 3 * HALF]
    right_state = (down - 0.5 * there)[0 : 3 * HALF]
    flux = jnp.dot(
        left_state, plus_ref[...], precision=lax.Precision.HIGHEST, preferred_element_type=jnp.float32
    ) + jnp.dot(
        right_state, minus_ref[...], precision=lax.Precision.HIGHEST, preferred_element_type=jnp.float32
    )
    change = pltpu.roll(flux, 1, 0) - flux
    base[...] = own.astype(jnp.float32) + 0.4 * change[HALF : 3 * HALF]

    def x_in(q):
        remote(block(q), block(q), x_send.at[q], x_recv.at[q], me).wait_recv()

    for q in order:
        x_in(q)
        go(first(q))
    second_in(0)
    go([paired(0, core)])
    first_in(order[0])
    go(second(order[0]))
    for load in loads:
        load.wait()
    spot_of = [mod(pair_table[spec, t], species) for t in range(species)]

    def exits(q):
        copies = []
        for j in range(plane):
            if q == 0 and j == 0:
                continue
            d = mod(spot + j, plane)
            to = (mod(x + q, nx) * plane + d, spec)
            copies.append(
                remote(outgoing.at[q, d], incoming.at[cell], exit_send.at[q, j], exit_recv.at[q, j], to)
            )
        return copies

    chunks = (0,) + order
    parts = out_modes // GROUP
    for at, q in enumerate(chunks):
        paired(q, 1 - core).wait_recv()
        own_t[...] = jnp.transpose(
            held[q][core, yl].reshape(plane * 2 * HALF, modes).astype(jnp.float32)
        )
        for g in range(parts):
            pieces = [held[q][t % ncore, t // ncore].reshape(plane * 2 * HALF, modes) for t in range(species)]
            right = jnp.concatenate(pieces, axis=1)
            left = jnp.concatenate(
                [
                    jnp.concatenate([a_ref[spot_of[t], GROUP * g + u] for t in range(species)], axis=1)
                    for u in range(GROUP)
                ],
                axis=0,
            )
            inner = lax.dot_general(
                left, right, (((1,), (1,)), ((), ())), preferred_element_type=jnp.float32
            )
            for u in range(GROUP):
                k = GROUP * g + u
                rows[k : k + 1, :] = jnp.sum(
                    inner[modes * u : modes * (u + 1)] * own_t[...], axis=0, keepdims=True
                )
            if g == 0 and at + 1 < len(chunks):
                second_in(chunks[at + 1])
                go([paired(chunks[at + 1], core)])
            if g == 0 and at + 2 < len(chunks):
                first_in(chunks[at + 2])
                go(second(chunks[at + 2]))
        whole = rows[...]
        width = plane * 2 * HALF
        for d in range(plane):
            turned = whole if d == 0 else pltpu.roll(whole, width - 2 * HALF * d, 1)
            outgoing[q, d] = turned[:, 0:128]
        go(exits(q))
    incoming[cell] = outgoing[0, spot]
    for q in range(nx):
        for j in range(plane):
            if q == 0 and j == 0:
                continue
            source = mod(x + nx - q, nx) * plane + mod(spot + plane - j, plane)
            slot = incoming.at[source]
            remote(slot, slot, exit_send.at[q, j], exit_recv.at[q, j], me).wait_recv()
    table = jnp.concatenate([incoming[i] for i in range(ring)], axis=0)
    collision = jnp.transpose(table)[0 : 2 * HALF]
    coll_ref[0] = collision
    new_ref[0] = base[...] + 0.5 * collision
    for copy in sent:
        copy.wait_send()


def local(dims, fields, tensors, pair_table, plus_flux, minus_flux, face_limiter):
    nx, nz, nyh, nyl, ncore = dims
    _, cells, modes = fields.shape
    out_modes = tensors.shape[1]
    plane = nz * nyh
    ring = nx * plane
    width = plane * cells
    dma = pltpu.SemaphoreType.DMA
    held = pltpu.VMEM((ncore, nyl, nz, nyh, 2, HALF, modes), jnp.bfloat16)
    any_space = pl.BlockSpec(memory_space=pl.ANY)
    fields = fields.reshape(1, 2, HALF, modes)
    return pl.pallas_call(
        functools.partial(step_kernel, dims),
        out_shape=(
            jax.ShapeDtypeStruct((1, cells, modes), jnp.float32),
            jax.ShapeDtypeStruct((1, cells, modes), jnp.float32),
        ),
        in_specs=[pl.BlockSpec(memory_space=pltpu.SMEM)] + [any_space] * 5,
        out_specs=(pl.BlockSpec(memory_space=pltpu.VMEM),) * 2,
        scratch_shapes=[
            held,
            held,
            held,
            held,
            pltpu.VMEM(tensors.shape, jnp.bfloat16),
            pltpu.VMEM((modes, modes), jnp.float32),
            pltpu.VMEM((modes, modes), jnp.float32),
            pltpu.VMEM((1, cells), jnp.int32),
            pltpu.VMEM((1, cells), jnp.int32),
            pltpu.VMEM((HALF, modes), jnp.bfloat16),
            pltpu.VMEM((HALF, modes), jnp.bfloat16),
            pltpu.VMEM((modes, width), jnp.float32),
            pltpu.VMEM((8, 128), jnp.float32),
            pltpu.VMEM((nx, plane, out_modes, 128), jnp.float32),
            pltpu.VMEM((ring, out_modes, 128), jnp.float32),
            pltpu.VMEM((out_modes, width), jnp.float32),
            pltpu.VMEM((cells, modes), jnp.float32),
            dma((8,)),
            dma((3,)),
            dma((3,)),
            dma((nx,)),
            dma((nx,)),
            dma((nx, 12)),
            dma((nx, 12)),
            dma((nx,)),
            dma((nx,)),
            dma((nx, plane)),
            dma((nx, plane)),
        ],
        compiler_params=pltpu.CompilerParams(
            collective_id=0, has_side_effects=True, vmem_limit_bytes=60 * 2**20
        ),
        name="step",
    )(pair_table, fields, tensors, plus_flux, minus_flux, face_limiter)


def solution(mesh):
    placed = (
        P("spec", "cell", None),
        P("spec", "cell", None, None),
        P(),
        P("spec", None, None),
        P("spec", None, None),
        P("spec", "cell"),
    )
    dims = (4, 4, 2, 2, 2)
    return jax.shard_map(
        functools.partial(local, dims),
        mesh=mesh,
        in_specs=placed,
        out_specs=(P("spec", "cell", None), P("spec", "cell", None)),
        check_vma=False,
    )
```

```python
import functools

import jax
import jax.numpy as jnp
from jax import lax
from jax.experimental import pallas as pl
from jax.experimental.pallas import tpu as pltpu
from jax.sharding import PartitionSpec as P

MESH = pl.DeviceIdType.MESH
HALF = 16
GROUP = 4
STRETCHES = ((0,), (2, 1), (3,))


def minmod_two(first, second):
    least = jnp.minimum(jnp.abs(first), jnp.abs(second))
    return jnp.where(first * second > 0, jnp.where(first > 0, least, -least), 0.0)


def minmod_three(first, second, third):
    same = (first * second > 0) & (second * third > 0)
    least = jnp.minimum(jnp.minimum(jnp.abs(first), jnp.abs(second)), jnp.abs(third))
    return jnp.where(same, jnp.where(first > 0, least, -least), 0.0)


def mod(value, size):
    return lax.rem(value, size)


def step_kernel(
    dims,
    table_hbm,
    fields,
    tensors,
    plus_hbm,
    minus_hbm,
    limiter,
    new_ref,
    coll_ref,
    held0,
    held1,
    held2,
    held3,
    a_ref,
    plus_ref,
    minus_ref,
    flag_ref,
    prior_flag,
    before,
    after,
    own_t,
    line,
    outgoing,
    incoming,
    rows,
    base,
    pair_table,
    load_sem,
    edge_send,
    edge_recv,
    x_send,
    x_recv,
    line_send,
    line_recv,
    pair_send,
    pair_recv,
    exit_send,
    exit_recv,
):
    nx, nz, nyh, nyl, ncore = dims
    ny = nyh * nyl
    held = (held0, held1, held2, held3)
    species = nyl * ncore
    out_modes = tensors.shape[1]
    modes = tensors.shape[2]
    plane = nz * nyh
    cell = lax.axis_index("cell")
    spec = lax.axis_index("spec")
    yh = mod(cell, nyh)
    z = mod(lax.div(cell, nyh), nz)
    x = lax.div(cell, plane)
    spot = mod(cell, plane)
    yl = lax.div(spec, ncore)
    core = mod(spec, ncore)
    y = yh * nyl + yl

    def device(x_at, z_at, y_at, core_at):
        return (
            (x_at * nz + z_at) * nyh + lax.div(y_at, nyl),
            mod(y_at, nyl) * ncore + core_at,
        )

    def remote(src, dst, send, recv, to):
        return pltpu.make_async_remote_copy(
            src_ref=src,
            dst_ref=dst,
            send_sem=send,
            recv_sem=recv,
            device_id=to,
            device_id_type=MESH,
        )

    def block(q):
        return held[q].at[core, yl, z, yh]

    loads = [
        pltpu.make_async_copy(tensors.at[p], a_ref.at[p], load_sem.at[p])
        for p in range(species)
    ]
    own_load = pltpu.make_async_copy(fields.at[0], block(0), load_sem.at[4])
    flag_load = pltpu.make_async_copy(limiter, flag_ref, load_sem.at[5])
    plus_load = pltpu.make_async_copy(plus_hbm.at[0], plus_ref, load_sem.at[6])
    minus_load = pltpu.make_async_copy(minus_hbm.at[0], minus_ref, load_sem.at[7])
    table_load = pltpu.make_async_copy(table_hbm, pair_table, load_sem.at[8])
    own_load.start()
    flag_load.start()
    plus_load.start()
    minus_load.start()
    table_load.start()
    for load in loads:
        load.start()

    ring = nx * plane
    succ = (mod(cell + 1, ring), spec)
    pred = (mod(cell + ring - 1, ring), spec)
    greeted = [device(x, z, y, 1 - core), succ, pred]
    greeted += [device(mod(x + o, nx), z, y, core) for o in range(1, nx)]
    greeted += [device(x, mod(z + o, nz), y, core) for o in range(1, nz)]
    greeted += [device(x, z, mod(y + o, ny), core) for o in range(1, ny)]
    barrier = pltpu.get_barrier_semaphore()
    for other in greeted:
        pl.semaphore_signal(barrier, inc=1, device_id=other, device_id_type=MESH)
    own_load.wait()
    flag_load.wait()
    pl.semaphore_wait(barrier, len(greeted))

    def first(q):
        copies = []
        for o in range(1, ny):
            here = held[q].at[core, yl, z, yh, 0]
            to = device(x, z, mod(y + o, ny), core)
            copies.append((here, here, line_send.at[q, o - 1], line_recv.at[q, o - 1], to))
        for o in range(1, nz):
            here = held[q].at[core, yl, z, yh, 1]
            to = device(x, mod(z + o, nz), y, core)
            copies.append((here, here, line_send.at[q, o + 2], line_recv.at[q, o + 2], to))
        return [remote(*c) for c in copies]

    def second(q):
        copies = []
        for o in range(1, nz):
            here = held[q].at[core, :, z, :, 0]
            to = device(x, mod(z + o, nz), y, core)
            copies.append((here, here, line_send.at[q, o + 5], line_recv.at[q, o + 5], to))
        for o in range(1, ny):
            here = held[q].at[core, yl, :, yh, 1]
            to = device(x, z, mod(y + o, ny), core)
            copies.append((here, here, line_send.at[q, o + 8], line_recv.at[q, o + 8], to))
        return [remote(*c) for c in copies]

    def first_in(q):
        me = (cell, spec)
        for o in range(1, ny):
            y_from = mod(y + ny - o, ny)
            there = held[q].at[core, mod(y_from, nyl), z, lax.div(y_from, nyl), 0]
            remote(there, there, line_send.at[q, o - 1], line_recv.at[q, o - 1], me).wait_recv()
        for o in range(1, nz):
            there = held[q].at[core, yl, mod(z + nz - o, nz), yh, 1]
            remote(there, there, line_send.at[q, o + 2], line_recv.at[q, o + 2], me).wait_recv()

    def second_in(q):
        me = (cell, spec)
        for o in range(1, nz):
            there = held[q].at[core, :, mod(z + nz - o, nz), :, 0]
            remote(there, there, line_send.at[q, o + 5], line_recv.at[q, o + 5], me).wait_recv()
        for o in range(1, ny):
            y_from = mod(y + ny - o, ny)
            there = held[q].at[core, mod(y_from, nyl), :, lax.div(y_from, nyl), 1]
            remote(there, there, line_send.at[q, o + 8], line_recv.at[q, o + 8], me).wait_recv()

    def paired(q, which):
        half = held[q].at[which]
        return remote(half, half, pair_send.at[q], pair_recv.at[q], device(x, z, y, 1 - core))

    sent = []

    def go(copies):
        for copy in copies:
            copy.start()
        sent.extend(copies)

    me = (cell, spec)

    def x_out(q):
        to = device(mod(x + nx - q, nx), z, y, core)
        return remote(block(0), block(q), x_send.at[q], x_recv.at[q], to)

    def x_in(q):
        remote(block(q), block(q), x_send.at[q], x_recv.at[q], me).wait_recv()

    far = sum(STRETCHES[1:], ())
    go(first(0))
    go([x_out(q) for q in far])
    first_in(0)
    go(second(0))
    for q in far:
        x_in(q)
        go(first(q))
    go(
        [
            remote(held[0].at[core, yl, z, yh, 1], before, edge_send.at[0], edge_recv.at[0], succ),
            remote(held[0].at[core, yl, z, yh, 0], after, edge_send.at[1], edge_recv.at[1], pred),
            remote(flag_ref, prior_flag, edge_send.at[2], edge_recv.at[2], succ),
        ]
    )
    second_in(0)
    go([paired(0, core)])
    for q in far:
        first_in(q)
        go(second(q))
    table_load.wait()
    for load in loads:
        load.wait()
    spot_of = [mod(pair_table[spec, t], species) for t in range(species)]

    def exits(q):
        copies = []
        for j in range(plane):
            if q == 0 and j == 0:
                continue
            d = mod(spot + j, plane)
            to = (mod(x + q, nx) * plane + d, spec)
            copies.append(
                remote(outgoing.at[q, d], incoming.at[cell], exit_send.at[q, j], exit_recv.at[q, j], to)
            )
        return copies

    parts = out_modes // GROUP
    width = plane * 2 * HALF
    for at, stretch in enumerate(STRETCHES):
        if at == 1:
            for q in far:
                second_in(q)
                go([paired(q, core)])
        for q in stretch:
            paired(q, 1 - core).wait_recv()
        for q in stretch:
            own_t[q] = jnp.transpose(held[q][core, yl].reshape(width, modes).astype(jnp.float32))
            pieces = [held[q][t % ncore, t // ncore].reshape(width, modes) for t in range(species)]
            right = jnp.concatenate(pieces, axis=1)
            for g in range(parts):
                left = jnp.concatenate(
                    [
                        jnp.concatenate([a_ref[spot_of[t], GROUP * g + u] for t in range(species)], axis=1)
                        for u in range(GROUP)
                    ],
                    axis=0,
                )
                inner = lax.dot_general(
                    left, right, (((1,), (1,)), ((), ())), preferred_element_type=jnp.float32
                )
                for u in range(GROUP):
                    k = GROUP * g + u
                    rows[q, k : k + 1, :] = jnp.sum(
                        inner[modes * u : modes * (u + 1)] * own_t[q], axis=0, keepdims=True
                    )
            whole = rows[q]
            for d in range(plane):
                turned = whole if d == 0 else pltpu.roll(whole, width - 2 * HALF * d, 1)
                outgoing[q, d] = turned[:, 0:128]
        for q in stretch:
            go(exits(q))
    plus_load.wait()
    minus_load.wait()
    remote(before, before, edge_send.at[0], edge_recv.at[0], me).wait_recv()
    remote(after, after, edge_send.at[1], edge_recv.at[1], me).wait_recv()
    remote(flag_ref, prior_flag, edge_send.at[2], edge_recv.at[2], me).wait_recv()
    own = held[0][core, yl, z, yh].reshape(2 * HALF, modes)
    wide = jnp.concatenate([before[...], own, after[...]], axis=0).astype(jnp.float32)
    count = 4 * HALF
    up = pltpu.roll(wide, 1, 0)
    down = pltpu.roll(wide, count - 1, 0)
    lower = wide - up
    upper = down - wide
    slope_one = minmod_two(lower, upper)
    slope_two = minmod_three(2.0 * lower, 0.5 * (lower + upper), 2.0 * upper)
    line[...] = jnp.zeros_like(line)
    line[0:1, 0 : 2 * HALF] = flag_ref[...].astype(jnp.float32)
    line[1:2, 0 : 2 * HALF] = prior_flag[...].astype(jnp.float32)
    columns = jnp.transpose(line[...])
    flags = jnp.concatenate(
        [
            columns[HALF : 2 * HALF, 1:2],
            columns[0 : 2 * HALF, 0:1],
            jnp.zeros((HALF, 1), jnp.float32),
        ],
        axis=0,
    )
    flags = jnp.broadcast_to(flags, (count, modes))
    here = jnp.where(flags == 1.0, slope_one, jnp.where(flags == 2.0, slope_two, 0.0))
    next_one = pltpu.roll(slope_one, count - 1, 0)
    next_two = pltpu.roll(slope_two, count - 1, 0)
    there = jnp.where(flags == 1.0, next_one, jnp.where(flags == 2.0, next_two, 0.0))
    left_state = (wide + 0.5 * here)[0 : 3 * HALF]
    right_state = (down - 0.5 * there)[0 : 3 * HALF]
    flux = jnp.dot(
        left_state, plus_ref[...], precision=lax.Precision.HIGHEST, preferred_element_type=jnp.float32
    ) + jnp.dot(
        right_state, minus_ref[...], precision=lax.Precision.HIGHEST, preferred_element_type=jnp.float32
    )
    change = pltpu.roll(flux, 1, 0) - flux
    base[...] = own.astype(jnp.float32) + 0.4 * change[HALF : 3 * HALF]


    incoming[cell] = outgoing[0, spot]
    for q in range(nx):
        for j in range(plane):
            if q == 0 and j == 0:
                continue
            source = mod(x + nx - q, nx) * plane + mod(spot + plane - j, plane)
            slot = incoming.at[source]
            remote(slot, slot, exit_send.at[q, j], exit_recv.at[q, j], me).wait_recv()
    table = jnp.concatenate([incoming[i] for i in range(ring)], axis=0)
    collision = jnp.transpose(table)[0 : 2 * HALF]
    coll_ref[0] = collision
    new_ref[0] = base[...] + 0.5 * collision
    for copy in sent:
        copy.wait_send()


def local(dims, fields, tensors, pair_table, plus_flux, minus_flux, face_limiter):
    nx, nz, nyh, nyl, ncore = dims
    _, cells, modes = fields.shape
    out_modes = tensors.shape[1]
    plane = nz * nyh
    ring = nx * plane
    width = plane * cells
    dma = pltpu.SemaphoreType.DMA
    held = pltpu.VMEM((ncore, nyl, nz, nyh, 2, HALF, modes), jnp.bfloat16)
    in_hbm = pl.BlockSpec(memory_space=pltpu.HBM)
    fields = fields.reshape(1, 2, HALF, modes)
    operands = (pair_table, fields, tensors, plus_flux, minus_flux, face_limiter)
    return pl.pallas_call(
        functools.partial(step_kernel, dims),
        out_shape=(
            jax.ShapeDtypeStruct((1, cells, modes), jnp.float32),
            jax.ShapeDtypeStruct((1, cells, modes), jnp.float32),
        ),
        in_specs=[in_hbm] * 6,
        out_specs=(pl.BlockSpec(memory_space=pltpu.VMEM),) * 2,
        scratch_shapes=[
            held,
            held,
            held,
            held,
            pltpu.VMEM(tensors.shape, jnp.bfloat16),
            pltpu.VMEM((modes, modes), jnp.float32),
            pltpu.VMEM((modes, modes), jnp.float32),
            pltpu.VMEM((1, cells), jnp.int32),
            pltpu.VMEM((1, cells), jnp.int32),
            pltpu.VMEM((HALF, modes), jnp.bfloat16),
            pltpu.VMEM((HALF, modes), jnp.bfloat16),
            pltpu.VMEM((nx, modes, width), jnp.float32),
            pltpu.VMEM((8, 128), jnp.float32),
            pltpu.VMEM((nx, plane, out_modes, 128), jnp.float32),
            pltpu.VMEM((ring, out_modes, 128), jnp.float32),
            pltpu.VMEM((nx, out_modes, width), jnp.float32),
            pltpu.VMEM((cells, modes), jnp.float32),
            pltpu.SMEM(pair_table.shape, jnp.int32),
            dma((9,)),
            dma((3,)),
            dma((3,)),
            dma((nx,)),
            dma((nx,)),
            dma((nx, 12)),
            dma((nx, 12)),
            dma((nx,)),
            dma((nx,)),
            dma((nx, plane)),
            dma((nx, plane)),
        ],
        compiler_params=pltpu.CompilerParams(
            collective_id=0, has_side_effects=True, vmem_limit_bytes=40 * 2**20
        ),
        name="step",
    )(*[pltpu.with_memory_space_constraint(v, pltpu.HBM) for v in operands])


def solution(mesh):
    placed = (
        P("spec", "cell", None),
        P("spec", "cell", None, None),
        P(),
        P("spec", None, None),
        P("spec", None, None),
        P("spec", "cell"),
    )
    dims = (4, 4, 2, 2, 2)
    return jax.shard_map(
        functools.partial(local, dims),
        mesh=mesh,
        in_specs=placed,
        out_specs=(P("spec", "cell", None), P("spec", "cell", None)),
        check_vma=False,
    )
```

```python
import functools

import jax
import jax.numpy as jnp
from jax import lax
from jax.experimental import pallas as pl
from jax.experimental.pallas import tpu as pltpu
from jax.sharding import PartitionSpec as P

MESH = pl.DeviceIdType.MESH
HALF = 16
GROUP = 3
FARTHEST = (2, 1, 3)


def minmod_two(first, second):
    least = jnp.minimum(jnp.abs(first), jnp.abs(second))
    return jnp.where(first * second > 0, jnp.where(first > 0, least, -least), 0.0)


def minmod_three(first, second, third):
    same = (first * second > 0) & (second * third > 0)
    least = jnp.minimum(jnp.minimum(jnp.abs(first), jnp.abs(second)), jnp.abs(third))
    return jnp.where(same, jnp.where(first > 0, least, -least), 0.0)


def mod(value, size):
    return lax.rem(value, size)


def step_kernel(
    dims,
    table_hbm,
    fields,
    tensors,
    plus_hbm,
    minus_hbm,
    limiter,
    new_ref,
    coll_ref,
    held0,
    held1,
    held2,
    held3,
    a_ref,
    plus_ref,
    minus_ref,
    flag_ref,
    prior_flag,
    before,
    after,
    own_t,
    line,
    outgoing,
    incoming,
    rows,
    base,
    pair_table,
    load_sem,
    edge_send,
    edge_recv,
    x_send,
    x_recv,
    line_send,
    line_recv,
    pair_send,
    pair_recv,
    exit_send,
    exit_recv,
):
    nx, nz, nyh, nyl, ncore = dims
    ny = nyh * nyl
    held = (held0, held1, held2, held3)
    species = nyl * ncore
    out_modes = tensors.shape[1]
    modes = tensors.shape[2]
    plane = nz * nyh
    cell = lax.axis_index("cell")
    spec = lax.axis_index("spec")
    yh = mod(cell, nyh)
    z = mod(lax.div(cell, nyh), nz)
    x = lax.div(cell, plane)
    spot = mod(cell, plane)
    yl = lax.div(spec, ncore)
    core = mod(spec, ncore)
    y = yh * nyl + yl

    def device(x_at, z_at, y_at, core_at):
        return (
            (x_at * nz + z_at) * nyh + lax.div(y_at, nyl),
            mod(y_at, nyl) * ncore + core_at,
        )

    def remote(src, dst, send, recv, to):
        return pltpu.make_async_remote_copy(
            src_ref=src,
            dst_ref=dst,
            send_sem=send,
            recv_sem=recv,
            device_id=to,
            device_id_type=MESH,
        )

    def block(q):
        return held[q].at[core, yl, z, yh]

    loads = [
        pltpu.make_async_copy(tensors.at[p], a_ref.at[p], load_sem.at[p])
        for p in range(species)
    ]
    own_load = pltpu.make_async_copy(fields.at[0], block(0), load_sem.at[4])
    flag_load = pltpu.make_async_copy(limiter, flag_ref, load_sem.at[5])
    plus_load = pltpu.make_async_copy(plus_hbm.at[0], plus_ref, load_sem.at[6])
    minus_load = pltpu.make_async_copy(minus_hbm.at[0], minus_ref, load_sem.at[7])
    table_load = pltpu.make_async_copy(table_hbm, pair_table, load_sem.at[8])
    own_load.start()
    flag_load.start()
    plus_load.start()
    minus_load.start()
    table_load.start()
    for load in loads:
        load.start()

    ring = nx * plane
    succ = (mod(cell + 1, ring), spec)
    pred = (mod(cell + ring - 1, ring), spec)
    greeted = [device(x, z, y, 1 - core), succ, pred]
    greeted += [device(mod(x + o, nx), z, y, core) for o in range(1, nx)]
    greeted += [device(x, mod(z + o, nz), y, core) for o in range(1, nz)]
    greeted += [device(x, z, mod(y + o, ny), core) for o in range(1, ny)]
    barrier = pltpu.get_barrier_semaphore()
    for other in greeted:
        pl.semaphore_signal(barrier, inc=1, device_id=other, device_id_type=MESH)
    own_load.wait()
    flag_load.wait()
    pl.semaphore_wait(barrier, len(greeted))

    def first(q):
        copies = []
        for o in FARTHEST:
            here = held[q].at[core, yl, z, yh, 0]
            to = device(x, z, mod(y + o, ny), core)
            copies.append((here, here, line_send.at[q, o - 1], line_recv.at[q, o - 1], to))
        for o in FARTHEST:
            here = held[q].at[core, yl, z, yh, 1]
            to = device(x, mod(z + o, nz), y, core)
            copies.append((here, here, line_send.at[q, o + 2], line_recv.at[q, o + 2], to))
        return [remote(*c) for c in copies]

    def second(q):
        copies = []
        for o in FARTHEST:
            here = held[q].at[core, :, z, :, 0]
            to = device(x, mod(z + o, nz), y, core)
            copies.append((here, here, line_send.at[q, o + 5], line_recv.at[q, o + 5], to))
        for o in FARTHEST:
            here = held[q].at[core, yl, :, yh, 1]
            to = device(x, z, mod(y + o, ny), core)
            copies.append((here, here, line_send.at[q, o + 8], line_recv.at[q, o + 8], to))
        return [remote(*c) for c in copies]

    def first_in(q):
        me = (cell, spec)
        for o in range(1, ny):
            y_from = mod(y + ny - o, ny)
            there = held[q].at[core, mod(y_from, nyl), z, lax.div(y_from, nyl), 0]
            remote(there, there, line_send.at[q, o - 1], line_recv.at[q, o - 1], me).wait_recv()
        for o in range(1, nz):
            there = held[q].at[core, yl, mod(z + nz - o, nz), yh, 1]
            remote(there, there, line_send.at[q, o + 2], line_recv.at[q, o + 2], me).wait_recv()

    def second_in(q):
        me = (cell, spec)
        for o in range(1, nz):
            there = held[q].at[core, :, mod(z + nz - o, nz), :, 0]
            remote(there, there, line_send.at[q, o + 5], line_recv.at[q, o + 5], me).wait_recv()
        for o in range(1, ny):
            y_from = mod(y + ny - o, ny)
            there = held[q].at[core, mod(y_from, nyl), :, lax.div(y_from, nyl), 1]
            remote(there, there, line_send.at[q, o + 8], line_recv.at[q, o + 8], me).wait_recv()

    def paired(q, which):
        half = held[q].at[which]
        return remote(half, half, pair_send.at[q], pair_recv.at[q], device(x, z, y, 1 - core))

    sent = []

    def go(copies):
        for copy in copies:
            copy.start()
        sent.extend(copies)

    me = (cell, spec)

    def x_out(q):
        to = device(mod(x + nx - q, nx), z, y, core)
        return remote(block(0), block(q), x_send.at[q], x_recv.at[q], to)

    def x_in(q):
        remote(block(q), block(q), x_send.at[q], x_recv.at[q], me).wait_recv()

    chunks = (0, 2, 1, 3)
    far = chunks[1:]
    go(first(0))
    go([x_out(q) for q in far])
    first_in(0)
    go(second(0))
    for q in far:
        x_in(q)
        go(first(q))
    go(
        [
            remote(held[0].at[core, yl, z, yh, 1], before, edge_send.at[0], edge_recv.at[0], succ),
            remote(held[0].at[core, yl, z, yh, 0], after, edge_send.at[1], edge_recv.at[1], pred),
            remote(flag_ref, prior_flag, edge_send.at[2], edge_recv.at[2], succ),
        ]
    )
    second_in(0)
    go([paired(0, core)])
    for q in far:
        first_in(q)
        go(second(q))
    table_load.wait()
    for load in loads:
        load.wait()
    spot_of = [mod(pair_table[spec, t], species) for t in range(species)]

    def exits(q):
        copies = []
        for j in range(plane):
            if q == 0 and j == 0:
                continue
            d = mod(spot + j, plane)
            to = (mod(x + q, nx) * plane + d, spec)
            copies.append(
                remote(outgoing.at[q, d], incoming.at[cell], exit_send.at[q, j], exit_recv.at[q, j], to)
            )
        return copies

    parts = out_modes // GROUP
    width = plane * 2 * HALF
    paired(0, 1 - core).wait_recv()
    for at, q in enumerate(chunks):
        own_t[q] = jnp.transpose(held[q][core, yl].reshape(width, modes).astype(jnp.float32))
        pieces = [held[q][t % ncore, t // ncore].reshape(width, modes) for t in range(species)]
        right = jnp.concatenate(pieces, axis=1)
        for g in range(parts):
            left = jnp.concatenate(
                [
                    jnp.concatenate([a_ref[spot_of[t], GROUP * g + u] for t in range(species)], axis=1)
                    for u in range(GROUP)
                ],
                axis=0,
            )
            inner = lax.dot_general(
                left, right, (((1,), (1,)), ((), ())), preferred_element_type=jnp.float32
            )
            for u in range(GROUP):
                k = GROUP * g + u
                rows[q, k : k + 1, :] = jnp.sum(
                    inner[modes * u : modes * (u + 1)] * own_t[q], axis=0, keepdims=True
                )
            if g == 1 and at < 2:
                for later in chunks[1:2] if at == 0 else chunks[2:]:
                    second_in(later)
                    go([paired(later, core)])
        whole = rows[q]
        for d in range(plane):
            turned = whole if d == 0 else pltpu.roll(whole, width - 2 * HALF * d, 1)
            outgoing[q, d] = turned[:, 0:128]
        go(exits(q))
        if at + 1 < len(chunks):
            paired(chunks[at + 1], 1 - core).wait_recv()
    plus_load.wait()
    minus_load.wait()
    remote(before, before, edge_send.at[0], edge_recv.at[0], me).wait_recv()
    remote(after, after, edge_send.at[1], edge_recv.at[1], me).wait_recv()
    remote(flag_ref, prior_flag, edge_send.at[2], edge_recv.at[2], me).wait_recv()
    own = held[0][core, yl, z, yh].reshape(2 * HALF, modes)
    wide = jnp.concatenate([before[...], own, after[...]], axis=0).astype(jnp.float32)
    count = 4 * HALF
    up = pltpu.roll(wide, 1, 0)
    down = pltpu.roll(wide, count - 1, 0)
    lower = wide - up
    upper = down - wide
    slope_one = minmod_two(lower, upper)
    slope_two = minmod_three(2.0 * lower, 0.5 * (lower + upper), 2.0 * upper)
    line[...] = jnp.zeros_like(line)
    line[0:1, 0 : 2 * HALF] = flag_ref[...].astype(jnp.float32)
    line[1:2, 0 : 2 * HALF] = prior_flag[...].astype(jnp.float32)
    columns = jnp.transpose(line[...])
    flags = jnp.concatenate(
        [
            columns[HALF : 2 * HALF, 1:2],
            columns[0 : 2 * HALF, 0:1],
            jnp.zeros((HALF, 1), jnp.float32),
        ],
        axis=0,
    )
    flags = jnp.broadcast_to(flags, (count, modes))
    here = jnp.where(flags == 1.0, slope_one, jnp.where(flags == 2.0, slope_two, 0.0))
    next_one = pltpu.roll(slope_one, count - 1, 0)
    next_two = pltpu.roll(slope_two, count - 1, 0)
    there = jnp.where(flags == 1.0, next_one, jnp.where(flags == 2.0, next_two, 0.0))
    left_state = (wide + 0.5 * here)[0 : 3 * HALF]
    right_state = (down - 0.5 * there)[0 : 3 * HALF]
    flux = jnp.dot(
        left_state, plus_ref[...], precision=lax.Precision.HIGHEST, preferred_element_type=jnp.float32
    ) + jnp.dot(
        right_state, minus_ref[...], precision=lax.Precision.HIGHEST, preferred_element_type=jnp.float32
    )
    change = pltpu.roll(flux, 1, 0) - flux
    base[...] = own.astype(jnp.float32) + 0.4 * change[HALF : 3 * HALF]


    incoming[cell] = outgoing[0, spot]
    for q in range(nx):
        for j in range(plane):
            if q == 0 and j == 0:
                continue
            source = mod(x + nx - q, nx) * plane + mod(spot + plane - j, plane)
            slot = incoming.at[source]
            remote(slot, slot, exit_send.at[q, j], exit_recv.at[q, j], me).wait_recv()
    table = jnp.concatenate([incoming[i] for i in range(ring)], axis=0)
    collision = jnp.transpose(table)[0 : 2 * HALF]
    coll_ref[0] = collision
    new_ref[0] = base[...]
    for copy in sent:
        copy.wait_send()


def finish(kept, collision, new_ref, coll_ref):
    coll_ref[...] = collision[...]
    new_ref[...] = kept[...] + 0.5 * collision[...]


def local(dims, fields, tensors, pair_table, plus_flux, minus_flux, face_limiter):
    nx, nz, nyh, nyl, ncore = dims
    _, cells, modes = fields.shape
    out_modes = tensors.shape[1]
    plane = nz * nyh
    ring = nx * plane
    width = plane * cells
    dma = pltpu.SemaphoreType.DMA
    held = pltpu.VMEM((ncore, nyl, nz, nyh, 2, HALF, modes), jnp.bfloat16)
    in_hbm = pl.BlockSpec(memory_space=pltpu.HBM)
    fields = fields.reshape(1, 2, HALF, modes)
    operands = (pair_table, fields, tensors, plus_flux, minus_flux, face_limiter)
    kept, collision = pl.pallas_call(
        functools.partial(step_kernel, dims),
        out_shape=(
            jax.ShapeDtypeStruct((1, cells, modes), jnp.float32),
            jax.ShapeDtypeStruct((1, cells, modes), jnp.float32),
        ),
        in_specs=[in_hbm] * 6,
        out_specs=(pl.BlockSpec(memory_space=pltpu.VMEM),) * 2,
        scratch_shapes=[
            held,
            held,
            held,
            held,
            pltpu.VMEM(tensors.shape, jnp.bfloat16),
            pltpu.VMEM((modes, modes), jnp.float32),
            pltpu.VMEM((modes, modes), jnp.float32),
            pltpu.VMEM((1, cells), jnp.int32),
            pltpu.VMEM((1, cells), jnp.int32),
            pltpu.VMEM((HALF, modes), jnp.bfloat16),
            pltpu.VMEM((HALF, modes), jnp.bfloat16),
            pltpu.VMEM((nx, modes, width), jnp.float32),
            pltpu.VMEM((8, 128), jnp.float32),
            pltpu.VMEM((nx, plane, out_modes, 128), jnp.float32),
            pltpu.VMEM((ring, out_modes, 128), jnp.float32),
            pltpu.VMEM((nx, out_modes, width), jnp.float32),
            pltpu.VMEM((cells, modes), jnp.float32),
            pltpu.SMEM(pair_table.shape, jnp.int32),
            dma((9,)),
            dma((3,)),
            dma((3,)),
            dma((nx,)),
            dma((nx,)),
            dma((nx, 12)),
            dma((nx, 12)),
            dma((nx,)),
            dma((nx,)),
            dma((nx, plane)),
            dma((nx, plane)),
        ],
        compiler_params=pltpu.CompilerParams(
            collective_id=0, has_side_effects=True, vmem_limit_bytes=40 * 2**20
        ),
        name="step",
    )(*[pltpu.with_memory_space_constraint(v, pltpu.HBM) for v in operands])
    return pl.pallas_call(
        finish,
        out_shape=(
            jax.ShapeDtypeStruct((1, cells, modes), jnp.float32),
            jax.ShapeDtypeStruct((1, cells, modes), jnp.float32),
        ),
        in_specs=[pl.BlockSpec(memory_space=pltpu.VMEM)] * 2,
        out_specs=(pl.BlockSpec(memory_space=pltpu.VMEM),) * 2,
        compiler_params=pltpu.CompilerParams(vmem_limit_bytes=2**20),
        name="finish",
    )(kept, collision)


def solution(mesh):
    placed = (
        P("spec", "cell", None),
        P("spec", "cell", None, None),
        P(),
        P("spec", None, None),
        P("spec", None, None),
        P("spec", "cell"),
    )
    dims = (4, 4, 2, 2, 2)
    return jax.shard_map(
        functools.partial(local, dims),
        mesh=mesh,
        in_specs=placed,
        out_specs=(P("spec", "cell", None), P("spec", "cell", None)),
        check_vma=False,
    )
```

```python
import functools

import jax
import jax.numpy as jnp
from jax import lax
from jax.experimental import pallas as pl
from jax.experimental.pallas import tpu as pltpu
from jax.sharding import PartitionSpec as P

MESH = pl.DeviceIdType.MESH
HALF = 16
WIDE = 3
FARTHEST = (2, 1, 3)


def minmod_two(first, second):
    least = jnp.minimum(jnp.abs(first), jnp.abs(second))
    return jnp.where(first * second > 0, jnp.where(first > 0, least, -least), 0.0)


def minmod_three(first, second, third):
    same = (first * second > 0) & (second * third > 0)
    least = jnp.minimum(jnp.minimum(jnp.abs(first), jnp.abs(second)), jnp.abs(third))
    return jnp.where(same, jnp.where(first > 0, least, -least), 0.0)


def mod(value, size):
    return lax.rem(value, size)


def step_kernel(
    dims,
    table_hbm,
    fields,
    tensors,
    plus_hbm,
    minus_hbm,
    limiter,
    new_ref,
    coll_ref,
    held0,
    held1,
    held2,
    held3,
    a_ref,
    plus_ref,
    minus_ref,
    flag_ref,
    prior_flag,
    before,
    after,
    own_t,
    line,
    outgoing,
    incoming,
    rows,
    base,
    pair_table,
    load_sem,
    edge_send,
    edge_recv,
    x_send,
    x_recv,
    line_send,
    line_recv,
    pair_send,
    pair_recv,
    exit_send,
    exit_recv,
):
    nx, nz, nyh, nyl, ncore = dims
    ny = nyh * nyl
    held = (held0, held1, held2, held3)
    species = nyl * ncore
    out_modes = tensors.shape[1]
    modes = tensors.shape[2]
    plane = nz * nyh
    cell = lax.axis_index("cell")
    spec = lax.axis_index("spec")
    yh = mod(cell, nyh)
    z = mod(lax.div(cell, nyh), nz)
    x = lax.div(cell, plane)
    spot = mod(cell, plane)
    yl = lax.div(spec, ncore)
    core = mod(spec, ncore)
    y = yh * nyl + yl

    def device(x_at, z_at, y_at, core_at):
        return (
            (x_at * nz + z_at) * nyh + lax.div(y_at, nyl),
            mod(y_at, nyl) * ncore + core_at,
        )

    def remote(src, dst, send, recv, to):
        return pltpu.make_async_remote_copy(
            src_ref=src,
            dst_ref=dst,
            send_sem=send,
            recv_sem=recv,
            device_id=to,
            device_id_type=MESH,
        )

    def block(q):
        return held[q].at[core, yl, z, yh]

    loads = [
        pltpu.make_async_copy(tensors.at[p], a_ref.at[p], load_sem.at[p])
        for p in range(species)
    ]
    own_load = pltpu.make_async_copy(fields.at[0], block(0), load_sem.at[4])
    flag_load = pltpu.make_async_copy(limiter, flag_ref, load_sem.at[5])
    plus_load = pltpu.make_async_copy(plus_hbm.at[0], plus_ref, load_sem.at[6])
    minus_load = pltpu.make_async_copy(minus_hbm.at[0], minus_ref, load_sem.at[7])
    table_load = pltpu.make_async_copy(table_hbm, pair_table, load_sem.at[8])
    own_load.start()
    flag_load.start()
    plus_load.start()
    minus_load.start()
    table_load.start()
    for load in loads:
        load.start()

    ring = nx * plane
    succ = (mod(cell + 1, ring), spec)
    pred = (mod(cell + ring - 1, ring), spec)
    greeted = [device(x, z, y, 1 - core), succ, pred]
    greeted += [device(mod(x + o, nx), z, y, core) for o in range(1, nx)]
    greeted += [device(x, mod(z + o, nz), y, core) for o in range(1, nz)]
    greeted += [device(x, z, mod(y + o, ny), core) for o in range(1, ny)]
    barrier = pltpu.get_barrier_semaphore()
    for other in greeted:
        pl.semaphore_signal(barrier, inc=1, device_id=other, device_id_type=MESH)
    own_load.wait()
    flag_load.wait()
    pl.semaphore_wait(barrier, len(greeted))

    def first(q):
        copies = []
        for o in FARTHEST:
            here = held[q].at[core, yl, z, yh, 0]
            to = device(x, z, mod(y + o, ny), core)
            copies.append((here, here, line_send.at[q, o - 1], line_recv.at[q, o - 1], to))
        for o in FARTHEST:
            here = held[q].at[core, yl, z, yh, 1]
            to = device(x, mod(z + o, nz), y, core)
            copies.append((here, here, line_send.at[q, o + 2], line_recv.at[q, o + 2], to))
        return [remote(*c) for c in copies]

    def second(q):
        copies = []
        for o in FARTHEST:
            here = held[q].at[core, :, z, :, 0]
            to = device(x, mod(z + o, nz), y, core)
            copies.append((here, here, line_send.at[q, o + 5], line_recv.at[q, o + 5], to))
        for o in FARTHEST:
            here = held[q].at[core, yl, :, yh, 1]
            to = device(x, z, mod(y + o, ny), core)
            copies.append((here, here, line_send.at[q, o + 8], line_recv.at[q, o + 8], to))
        return [remote(*c) for c in copies]

    def first_in(q):
        me = (cell, spec)
        for o in range(1, ny):
            y_from = mod(y + ny - o, ny)
            there = held[q].at[core, mod(y_from, nyl), z, lax.div(y_from, nyl), 0]
            remote(there, there, line_send.at[q, o - 1], line_recv.at[q, o - 1], me).wait_recv()
        for o in range(1, nz):
            there = held[q].at[core, yl, mod(z + nz - o, nz), yh, 1]
            remote(there, there, line_send.at[q, o + 2], line_recv.at[q, o + 2], me).wait_recv()

    def second_in(q):
        me = (cell, spec)
        for o in range(1, nz):
            there = held[q].at[core, :, mod(z + nz - o, nz), :, 0]
            remote(there, there, line_send.at[q, o + 5], line_recv.at[q, o + 5], me).wait_recv()
        for o in range(1, ny):
            y_from = mod(y + ny - o, ny)
            there = held[q].at[core, mod(y_from, nyl), :, lax.div(y_from, nyl), 1]
            remote(there, there, line_send.at[q, o + 8], line_recv.at[q, o + 8], me).wait_recv()

    def paired(q, which):
        half = held[q].at[which]
        return remote(half, half, pair_send.at[q], pair_recv.at[q], device(x, z, y, 1 - core))

    sent = []

    def go(copies):
        for copy in copies:
            copy.start()
        sent.extend(copies)

    me = (cell, spec)

    def x_out(q):
        to = device(mod(x + nx - q, nx), z, y, core)
        return remote(block(0), block(q), x_send.at[q], x_recv.at[q], to)

    def x_in(q):
        remote(block(q), block(q), x_send.at[q], x_recv.at[q], me).wait_recv()

    chunks = (0, 2, 1, 3)
    far = chunks[1:]
    go(first(0))
    go([x_out(q) for q in far])
    first_in(0)
    go(second(0))
    for q in far:
        x_in(q)
        go(first(q))
    go(
        [
            remote(held[0].at[core, yl, z, yh, 1], before, edge_send.at[0], edge_recv.at[0], succ),
            remote(held[0].at[core, yl, z, yh, 0], after, edge_send.at[1], edge_recv.at[1], pred),
            remote(flag_ref, prior_flag, edge_send.at[2], edge_recv.at[2], succ),
        ]
    )
    second_in(0)
    go([paired(0, core)])
    for q in far:
        first_in(q)
        go(second(q))
    table_load.wait()
    for load in loads:
        load.wait()

    def exits(q):
        copies = []
        for j in range(plane):
            if q == 0 and j == 0:
                continue
            d = mod(spot + j, plane)
            to = (mod(x + q, nx) * plane + d, spec)
            copies.append(
                remote(outgoing.at[q, d], incoming.at[cell], exit_send.at[q, j], exit_recv.at[q, j], to)
            )
        return copies

    width = plane * 2 * HALF
    def stretch(q, cores, size, fresh):
        pieces = [held[q][c, l].reshape(width, modes) for c in cores for l in range(nyl)]
        right = jnp.concatenate(pieces, axis=1)
        spots = [mod(pair_table[spec, l * ncore + c], species) for c in cores for l in range(nyl)]
        for g in range(out_modes // size):
            left = jnp.concatenate(
                [
                    jnp.concatenate([a_ref[spot, size * g + u] for spot in spots], axis=1)
                    for u in range(size)
                ],
                axis=0,
            )
            inner = lax.dot_general(
                left, right, (((1,), (1,)), ((), ())), preferred_element_type=jnp.float32
            )
            for u in range(size):
                k = size * g + u
                row = jnp.sum(inner[modes * u : modes * (u + 1)] * own_t[q], axis=0, keepdims=True)
                rows[q, k : k + 1, :] = row if fresh else rows[q, k : k + 1, :] + row

    for at, q in enumerate(chunks):
        if at == 1:
            second_in(q)
            go([paired(q, core)])
        if at > 1:
            paired(q, 1 - core).wait_recv()
        own_t[q] = jnp.transpose(held[q][core, yl].reshape(width, modes).astype(jnp.float32))
        if at < 2:
            stretch(q, (core,), WIDE, True)
            if at == 1:
                for later in chunks[2:]:
                    second_in(later)
                    go([paired(later, core)])
            paired(q, 1 - core).wait_recv()
            stretch(q, (1 - core,), WIDE, False)
        else:
            stretch(q, (0, 1), WIDE, True)
        whole = rows[q]
        for d in range(plane):
            turned = whole if d == 0 else pltpu.roll(whole, width - 2 * HALF * d, 1)
            outgoing[q, d] = turned[:, 0:128]
        go(exits(q))
    plus_load.wait()
    minus_load.wait()
    remote(before, before, edge_send.at[0], edge_recv.at[0], me).wait_recv()
    remote(after, after, edge_send.at[1], edge_recv.at[1], me).wait_recv()
    remote(flag_ref, prior_flag, edge_send.at[2], edge_recv.at[2], me).wait_recv()
    own = held[0][core, yl, z, yh].reshape(2 * HALF, modes)
    wide = jnp.concatenate([before[...], own, after[...]], axis=0).astype(jnp.float32)
    count = 4 * HALF
    up = pltpu.roll(wide, 1, 0)
    down = pltpu.roll(wide, count - 1, 0)
    lower = wide - up
    upper = down - wide
    slope_one = minmod_two(lower, upper)
    slope_two = minmod_three(2.0 * lower, 0.5 * (lower + upper), 2.0 * upper)
    line[...] = jnp.zeros_like(line)
    line[0:1, 0 : 2 * HALF] = flag_ref[...].astype(jnp.float32)
    line[1:2, 0 : 2 * HALF] = prior_flag[...].astype(jnp.float32)
    columns = jnp.transpose(line[...])
    flags = jnp.concatenate(
        [
            columns[HALF : 2 * HALF, 1:2],
            columns[0 : 2 * HALF, 0:1],
            jnp.zeros((HALF, 1), jnp.float32),
        ],
        axis=0,
    )
    flags = jnp.broadcast_to(flags, (count, modes))
    here = jnp.where(flags == 1.0, slope_one, jnp.where(flags == 2.0, slope_two, 0.0))
    next_one = pltpu.roll(slope_one, count - 1, 0)
    next_two = pltpu.roll(slope_two, count - 1, 0)
    there = jnp.where(flags == 1.0, next_one, jnp.where(flags == 2.0, next_two, 0.0))
    left_state = (wide + 0.5 * here)[0 : 3 * HALF]
    right_state = (down - 0.5 * there)[0 : 3 * HALF]
    flux = jnp.dot(
        left_state, plus_ref[...], precision=lax.Precision.HIGHEST, preferred_element_type=jnp.float32
    ) + jnp.dot(
        right_state, minus_ref[...], precision=lax.Precision.HIGHEST, preferred_element_type=jnp.float32
    )
    change = pltpu.roll(flux, 1, 0) - flux
    base[...] = own.astype(jnp.float32) + 0.4 * change[HALF : 3 * HALF]


    incoming[cell] = outgoing[0, spot]
    for q in range(nx):
        for j in range(plane):
            if q == 0 and j == 0:
                continue
            source = mod(x + nx - q, nx) * plane + mod(spot + plane - j, plane)
            slot = incoming.at[source]
            remote(slot, slot, exit_send.at[q, j], exit_recv.at[q, j], me).wait_recv()
    table = jnp.concatenate([incoming[i] for i in range(ring)], axis=0)
    collision = jnp.transpose(table)[0 : 2 * HALF]
    coll_ref[0] = collision
    new_ref[0] = base[...]
    for copy in sent:
        copy.wait_send()


def finish(kept, collision, new_ref, coll_ref):
    coll_ref[...] = collision[...]
    new_ref[...] = kept[...] + 0.5 * collision[...]


def local(dims, fields, tensors, pair_table, plus_flux, minus_flux, face_limiter):
    nx, nz, nyh, nyl, ncore = dims
    _, cells, modes = fields.shape
    out_modes = tensors.shape[1]
    plane = nz * nyh
    ring = nx * plane
    width = plane * cells
    dma = pltpu.SemaphoreType.DMA
    held = pltpu.VMEM((ncore, nyl, nz, nyh, 2, HALF, modes), jnp.bfloat16)
    in_hbm = pl.BlockSpec(memory_space=pltpu.HBM)
    fields = fields.reshape(1, 2, HALF, modes)
    operands = (pair_table, fields, tensors, plus_flux, minus_flux, face_limiter)
    kept, collision = pl.pallas_call(
        functools.partial(step_kernel, dims),
        out_shape=(
            jax.ShapeDtypeStruct((1, cells, modes), jnp.float32),
            jax.ShapeDtypeStruct((1, cells, modes), jnp.float32),
        ),
        in_specs=[in_hbm] * 6,
        out_specs=(pl.BlockSpec(memory_space=pltpu.VMEM),) * 2,
        scratch_shapes=[
            held,
            held,
            held,
            held,
            pltpu.VMEM(tensors.shape, jnp.bfloat16),
            pltpu.VMEM((modes, modes), jnp.float32),
            pltpu.VMEM((modes, modes), jnp.float32),
            pltpu.VMEM((1, cells), jnp.int32),
            pltpu.VMEM((1, cells), jnp.int32),
            pltpu.VMEM((HALF, modes), jnp.bfloat16),
            pltpu.VMEM((HALF, modes), jnp.bfloat16),
            pltpu.VMEM((nx, modes, width), jnp.float32),
            pltpu.VMEM((8, 128), jnp.float32),
            pltpu.VMEM((nx, plane, out_modes, 128), jnp.float32),
            pltpu.VMEM((ring, out_modes, 128), jnp.float32),
            pltpu.VMEM((nx, out_modes, width), jnp.float32),
            pltpu.VMEM((cells, modes), jnp.float32),
            pltpu.SMEM(pair_table.shape, jnp.int32),
            dma((9,)),
            dma((3,)),
            dma((3,)),
            dma((nx,)),
            dma((nx,)),
            dma((nx, 12)),
            dma((nx, 12)),
            dma((nx,)),
            dma((nx,)),
            dma((nx, plane)),
            dma((nx, plane)),
        ],
        compiler_params=pltpu.CompilerParams(
            collective_id=0, has_side_effects=True, vmem_limit_bytes=40 * 2**20
        ),
        name="step",
    )(*[pltpu.with_memory_space_constraint(v, pltpu.HBM) for v in operands])
    return pl.pallas_call(
        finish,
        out_shape=(
            jax.ShapeDtypeStruct((1, cells, modes), jnp.float32),
            jax.ShapeDtypeStruct((1, cells, modes), jnp.float32),
        ),
        in_specs=[pl.BlockSpec(memory_space=pltpu.VMEM)] * 2,
        out_specs=(pl.BlockSpec(memory_space=pltpu.VMEM),) * 2,
        compiler_params=pltpu.CompilerParams(vmem_limit_bytes=2**20),
        name="finish",
    )(kept, collision)


def solution(mesh):
    placed = (
        P("spec", "cell", None),
        P("spec", "cell", None, None),
        P(),
        P("spec", None, None),
        P("spec", None, None),
        P("spec", "cell"),
    )
    dims = (4, 4, 2, 2, 2)
    return jax.shard_map(
        functools.partial(local, dims),
        mesh=mesh,
        in_specs=placed,
        out_specs=(P("spec", "cell", None), P("spec", "cell", None)),
        check_vma=False,
    )
```
